128 devices in a mesh: dp: 8 (over x, core), seq: 16 (over z, y).
Axes of the slice: x: 4, y: 4, z: 4, core: 2. Of those that a mesh axis runs over, the one named last changes fastest.
Arguments:
- tokens: bfloat16 [8, 12288, 2560], P('dp', 'seq'), may hold values from -6 to 6
- w_xbc: bfloat16 [2560, 2816], P(('dp', 'seq')), may hold values from -0.125 to 0.125
- conv_weight: float32 [4, 2816], replicated, may hold values from -3 to 3
- conv_bias: float32 [2816], replicated, may hold values from -2 to 2
- a_log: float32 [40], replicated, may hold values from -13 to -3
- dt_in: float32 [8, 40, 12288], P('dp', None, 'seq'), may hold values from -2 to 98304
- d_skip: float32 [40], replicated, may hold values from 0.5 to 1.5
- norm_gain: float32 [2560], replicated, may hold values from 0.25 to 1.75
Outputs:
- normed: bfloat16 [8, 12288, 2560], P('dp', 'seq')
The draws below stay inside these ranges and needn't reach their ends.
All inputs are finite; a program needn't handle non-finite values.
Results may differ from the reference program's by a relative error of at most 0.012.
Values may be sent and summed in bfloat16 or wider, within the bound.
A program may use at most 128 MiB of HBM per device.

```python
import math
import jax
import jax.numpy as jnp
from jax import lax

D = 2560
H = 40
P_SIZE = 64
N = 128
CONV = 4
GROUP = 256
TOK_DEV = 768
DXBC = 2816
SEQLEN = 12288
DESIGNS = 8


def head_rates(key):
    key_class, key_fast, key_slow = jax.random.split(jax.random.fold_in(key, 11), 3)
    fast_share = 5
    is_fast = jax.random.randint(key_class, (H,), 0, 10) < fast_share
    fast_rate = jnp.exp(jax.random.uniform(key_fast, (H,), jnp.float32, math.log(1.0 / 50.0), math.log(1.0 / 30.0)))
    slow_rate = jnp.exp(jax.random.uniform(key_slow, (H,), jnp.float32, math.log(0.1), math.log(0.4))) / SEQLEN
    return jnp.where(is_fast, fast_rate, slow_rate)


def draw_a_log(key, part):
    return jnp.log(head_rates(key)).astype(jnp.float32)


def draw_dt_in(key, part):
    rates = head_rates(key)
    key_block, key_jitter, key_place, key_loss = jax.random.split(jax.random.fold_in(key, 23), 4)
    shard_count = SEQLEN // TOK_DEV
    block_factor = jnp.exp(jax.random.uniform(key_block, (DESIGNS, 1, shard_count, 1), jnp.float32, math.log(0.5), math.log(2.0)))
    jitter = jnp.exp(jax.random.uniform(key_jitter, (DESIGNS, H, shard_count, TOK_DEV), jnp.float32, math.log(0.5), math.log(2.0)))
    target = (block_factor * jitter).reshape(DESIGNS, H, SEQLEN)
    places = jax.random.randint(key_place, (DESIGNS, 2), 0, SEQLEN)
    hit = jnp.any(jnp.arange(SEQLEN)[None, None, :] == places[:, :, None], axis=1)
    loss = jax.random.uniform(key_loss, (DESIGNS, 1, SEQLEN), jnp.float32, 0.223, 0.693)
    target = jnp.where(hit[:, None, :], loss / rates[None, :, None], target)
    inverse = jnp.where(target > 20.0, target, jnp.log(jnp.expm1(jnp.minimum(target, 20.0))))
    return inverse.astype(jnp.float32)


def levels(stream_key, dims, shards, smallest, top_value):
    gain = 1.0
    for position, blocks in shards:
        draws = jax.random.uniform(jax.random.fold_in(jax.random.fold_in(stream_key, 6), position), (blocks,), jnp.float32, smallest / len(shards), top_value / len(shards))
        gain = gain * jnp.repeat(jnp.exp(draws), dims[position] // blocks).reshape((-1,) + (1,) * (len(dims) - 1 - position))
    return gain


def bell_draw(key, dims, width, limit, cuts=(), kind=jnp.bfloat16):
    array = width * jax.random.normal(key, dims, jnp.float32)
    if cuts:
        array = array * levels(key, dims, cuts, -0.22, 0.18)
    return jnp.clip(array, -limit, limit).astype(kind)


def setup_inputs(seed: int = 0) -> dict:
    key_of = jax.random.split(jax.random.key(seed), 9)
    return {
        "tokens": bell_draw(key_of[0], (DESIGNS, SEQLEN, D), 1.0, 6.0, ((0, 8), (1, 16))),
        "w_xbc": bell_draw(key_of[1], (D, DXBC), D ** -0.5, 0.125, ((0, 128),)),
        "conv_weight": bell_draw(key_of[2], (CONV, DXBC), 4 ** -0.5, 3.0, (), jnp.float32),
        "conv_bias": bell_draw(key_of[3], (DXBC,), 0.3, 2.0, (), jnp.float32),
        "a_log": draw_a_log(jax.random.fold_in(key_of[8], 71), 0),
        "dt_in": draw_dt_in(jax.random.fold_in(key_of[8], 71), 0),
        "d_skip": jnp.clip(jax.random.uniform(key_of[6], (H,), jnp.float32, 0.5, 1.5), 0.5, 1.5),
        "norm_gain": jnp.clip(1.0 + 0.15 * jax.random.normal(key_of[7], (H * P_SIZE,), jnp.float32), 0.25, 1.75),
    }


def span_terms(x_block, b_block, c_block, dt_block, decay_block):
    heads = dt_block.shape[0]
    length = dt_block.shape[1]
    x_heads = x_block.astype(jnp.float32).reshape(length, heads, -1)
    b_float = b_block.astype(jnp.float32)
    cumul = jnp.cumsum(decay_block, axis=1)
    spread = cumul[:, :, None] - cumul[:, None, :]
    lower = jnp.arange(length)[:, None] >= jnp.arange(length)[None, :]
    decay_mat = jnp.exp(jnp.where(lower[None], spread, -jnp.inf))
    scores = jnp.dot(c_block, b_block.T, preferred_element_type=jnp.float32)
    mixing = decay_mat * scores[None] * dt_block[:, None, :]
    y_inner = jnp.einsum('hij,jhp->ihp', mixing, x_heads, precision=lax.Precision.HIGH)
    tail_weight = jnp.exp(cumul[:, -1:] - cumul) * dt_block
    weighted = tail_weight.T[:, :, None] * x_heads
    span_state = jnp.einsum('jhp,jn->hpn', weighted, b_float, precision=lax.Precision.HIGH)
    return (y_inner, span_state, cumul[:, -1], cumul)

def design_pass(design_tokens, design_dt, w_xbc, conv_weight, conv_bias, a_log, d_skip, norm_gain):
    xbc = jnp.dot(design_tokens, w_xbc, preferred_element_type=jnp.float32).astype(jnp.bfloat16)
    padded = jnp.concatenate([jnp.zeros((CONV - 1, DXBC), jnp.bfloat16), xbc], axis=0)
    accum = conv_bias[None, :] + jnp.zeros((SEQLEN, DXBC), jnp.float32)
    for tap_index in range(CONV):
        accum = accum + conv_weight[tap_index][None, :] * padded[tap_index:tap_index + SEQLEN].astype(jnp.float32)
    conv_out = jax.nn.silu(accum).astype(jnp.bfloat16)
    width_x = H * P_SIZE
    x_all = conv_out[:, :width_x]
    b_all = conv_out[:, width_x:width_x + N]
    c_all = conv_out[:, width_x + N:]
    step_size = jax.nn.softplus(design_dt)
    log_decay = -jnp.exp(a_log)[:, None] * step_size
    blocks = SEQLEN // GROUP
    x_blocks = x_all.reshape(blocks, GROUP, width_x)
    b_blocks = b_all.reshape(blocks, GROUP, N)
    c_blocks = c_all.reshape(blocks, GROUP, N)
    dt_blocks = step_size.reshape(H, blocks, GROUP).transpose(1, 0, 2)
    decay_blocks = log_decay.reshape(H, blocks, GROUP).transpose(1, 0, 2)

    def advance(state, inputs):
        x_block, b_block, c_block, dt_block, decay_block = inputs
        y_inner, span_state, totals, cumul = span_terms(x_block, b_block, c_block, dt_block, decay_block)
        from_state = jnp.einsum('in,hpn->ihp', c_block.astype(jnp.float32), state, precision=lax.Precision.HIGH)
        y_block = y_inner + jnp.exp(cumul).T[:, :, None] * from_state
        new_state = jnp.exp(totals)[:, None, None] * state + span_state
        return (new_state, y_block)
    start_state = jnp.zeros((H, P_SIZE, N), jnp.float32)
    final_state, y_blocks = lax.scan(advance, start_state, (x_blocks, b_blocks, c_blocks, dt_blocks, decay_blocks))
    x_heads = x_all.astype(jnp.float32).reshape(SEQLEN, H, P_SIZE)
    ssd = y_blocks.reshape(SEQLEN, H, P_SIZE) + d_skip[None, :, None] * x_heads
    mean_sq = lax.optimization_barrier(jnp.mean(ssd * ssd, axis=-1, keepdims=True))
    scaled = ssd * lax.rsqrt(mean_sq + 1e-05) * norm_gain.reshape(H, P_SIZE)[None]
    return scaled.reshape(SEQLEN, H * P_SIZE).astype(jnp.bfloat16)

def reference(tokens, w_xbc, conv_weight, conv_bias, a_log, dt_in, d_skip, norm_gain):

    def one_design(pair):
        return design_pass(pair[0], pair[1], w_xbc, conv_weight, conv_bias, a_log, d_skip, norm_gain)
    return lax.map(one_design, (tokens, dt_in))
```

```python
import functools
import math

import jax
import jax.numpy as jnp
from jax import lax
from jax.experimental import pallas as pl
from jax.experimental.pallas import tpu as pltpu
from jax.sharding import PartitionSpec as P

Q = 128
LOG2E = math.log2(math.e)
F32 = jnp.float32
BF16 = jnp.bfloat16


def dot(a, b, precision=None):
    return lax.dot_general(
        a, b, (((1,), (0,)), ((), ())), precision=precision, preferred_element_type=F32
    )


def conv_silu(work, cw, cb, rows, pad):
    taps = cw.shape[0]
    acc = cb
    for k in range(taps):
        acc = acc + cw[k : k + 1, :] * work[pl.ds(pad - (taps - 1) + k, rows), :]
    half = 0.5 * acc
    return half + half * jnp.tanh(half)


def project_kernel(pad, tok_hbm, rim_hbm, w_ref, cw_ref, cb_ref, out_ref, tok, work, sems):
    rows = out_ref.shape[0]

    @pl.when(pl.program_id(0) == 0)
    def _():
        first = pltpu.make_async_copy(rim_hbm, tok.at[pl.ds(0, pad)], sems.at[0])
        second = pltpu.make_async_copy(tok_hbm, tok.at[pl.ds(pad, rows)], sems.at[1])
        first.start()
        second.start()
        first.wait()
        second.wait()

    xbc = dot(tok[...], w_ref[...])
    work[...] = xbc.astype(BF16).astype(F32)
    out_ref[...] = conv_silu(work, cw_ref[...], cb_ref[...], rows, pad).astype(BF16)


def project(tokens, rim, w, conv_weight, conv_bias):
    rows, depth = tokens.shape
    channels = w.shape[1]
    pad = rim.shape[0]
    wide = 256
    return pl.pallas_call(
        functools.partial(project_kernel, pad),
        out_shape=jax.ShapeDtypeStruct((rows, channels), BF16),
        grid=(channels // wide,),
        in_specs=[
            pl.BlockSpec(memory_space=pl.ANY),
            pl.BlockSpec(memory_space=pl.ANY),
            pl.BlockSpec((depth, wide), lambda i: (0, i)),
            pl.BlockSpec((conv_weight.shape[0], wide), lambda i: (0, i)),
            pl.BlockSpec((1, wide), lambda i: (0, i)),
        ],
        out_specs=pl.BlockSpec((rows, wide), lambda i: (0, i)),
        scratch_shapes=[
            pltpu.VMEM((rows + pad, depth), BF16),
            pltpu.VMEM((rows + pad, wide), F32),
            pltpu.SemaphoreType.DMA((2,)),
        ],
    )(tokens, rim, w, conv_weight, conv_bias[None, :])


def prepare(dt_ref, a_ref, cum_t, row, tail_t, base_t):
    heads, rows = dt_ref.shape
    v = dt_ref[...]
    dt = jnp.maximum(v, 0.0) + jnp.log1p(jnp.exp(-jnp.abs(v)))
    log_dt = jnp.log2(dt)
    decay = (-LOG2E * jnp.exp(a_ref[...])) * dt
    upper = (
        lax.broadcasted_iota(jnp.int32, (Q, Q), 0) <= lax.broadcasted_iota(jnp.int32, (Q, Q), 1)
    ).astype(F32)
    base = jnp.zeros((heads, 1), F32)
    for c in range(rows // Q):
        span = slice(c * Q, (c + 1) * Q)
        cum = dot(decay[:, span], upper, lax.Precision.HIGHEST)
        total = cum[:, Q - 1 :]
        cum_t[c] = cum.T
        row[c] = cum - log_dt[:, span]
        tail_t[c] = jnp.exp2(total - cum + log_dt[:, span]).T
        base_t[c] = jnp.exp2(cum + base).T
        base = base + total
    return base


def pair_of(left, right):
    half = lax.broadcasted_iota(jnp.int32, (left.shape[0], 128), 1) < 64
    return jnp.where(half, left, right)


def states_pass(conv_ref, cum_t, tail_t, state, saved, width, n):
    blocks = cum_t.shape[0]
    state[...] = jnp.zeros_like(state)

    def step(c, carry):
        rows = pl.ds(pl.multiple_of(c * Q, Q), Q)
        b_t = conv_ref[rows, width : width + n].T
        last = cum_t[c, Q - 1 : Q, :]
        tail = tail_t[c]
        for pair in range(width // 128):
            h = 2 * pair
            cols = slice(pair * 128, (pair + 1) * 128)
            x = conv_ref[rows, cols].astype(F32)
            wx = (x * pair_of(tail[:, h : h + 1], tail[:, h + 1 : h + 2])).astype(BF16)
            old = state[:, cols]
            saved[c, :, cols] = old.astype(BF16)
            keep = jnp.exp2(pair_of(last[:, h : h + 1], last[:, h + 1 : h + 2]))
            state[:, cols] = keep * old + dot(b_t, wx)
        return carry

    lax.fori_loop(0, blocks, step, 0)


def inner_pass(conv_ref, cum_t, row, saved, skip_ref, part, width, n):
    blocks = cum_t.shape[0]
    lower = lax.broadcasted_iota(jnp.int32, (Q, Q), 0) >= lax.broadcasted_iota(jnp.int32, (Q, Q), 1)
    left = lax.broadcasted_iota(jnp.int32, (Q, 128), 1) < 64

    def step(c, carry):
        rows = pl.ds(pl.multiple_of(c * Q, Q), Q)
        b = conv_ref[rows, width : width + n]
        cm = conv_ref[rows, width + n :]
        scores = jnp.where(
            lower,
            lax.dot_general(cm, b, (((1,), (1,)), ((), ())), preferred_element_type=F32),
            0.0,
        )
        cum = cum_t[c]
        for pair in range(width // 128):
            cols = slice(pair * 128, (pair + 1) * 128)
            x = conv_ref[rows, cols]
            mixes = []
            own = []
            for h in (2 * pair, 2 * pair + 1):
                mine = jnp.broadcast_to(cum[:, h : h + 1], (Q, 128))
                spread = jnp.where(lower, mine - row[c, h : h + 1, :], -jnp.inf)
                mixes.append((jnp.exp2(spread) * scores).astype(BF16))
                own.append(mine)
            zero = jnp.zeros_like(x)
            stack = jnp.concatenate([jnp.where(left, x, zero), jnp.where(left, zero, x)], axis=0)
            y = dot(jnp.concatenate(mixes, axis=1), stack)
            y = y + jnp.exp2(jnp.where(left, own[0], own[1])) * dot(cm, saved[c, :, cols])
            part[rows, cols] = y + skip_ref[:, cols] * x.astype(F32)
        return carry

    lax.fori_loop(0, blocks, step, 0)


def final_pass(conv_ref, base_t, incoming, part, gain_ref, out_ref, width, n):
    blocks = base_t.shape[0]
    ri = lax.broadcasted_iota(jnp.int32, (128, 128), 0)
    ci = lax.broadcasted_iota(jnp.int32, (128, 128), 1)
    mean_of = jnp.where((ri < 64) == (ci < 64), 1.0 / 64, 0.0).astype(BF16)

    def step(c, carry):
        rows = pl.ds(pl.multiple_of(c * Q, Q), Q)
        cm = conv_ref[rows, width + n :]
        base = base_t[c]
        for pair in range(width // 128):
            h = 2 * pair
            cols = slice(pair * 128, (pair + 1) * 128)
            scale = pair_of(base[:, h : h + 1], base[:, h + 1 : h + 2])
            y = part[rows, cols] + scale * dot(cm, incoming[:, cols])
            mean_sq = dot((y * y).astype(BF16), mean_of)
            out_ref[rows, cols] = (y * lax.rsqrt(mean_sq + 1e-5) * gain_ref[:, cols]).astype(BF16)
        return carry

    lax.fori_loop(0, blocks, step, 0)


def ssd_kernel(width, n, conv_ref, dt_ref, a_ref, skip_ref,
               part, state_out, total_out, base_t, cum_t, row, tail_t, saved, state):
    total = prepare(dt_ref, a_ref, cum_t, row, tail_t, base_t)
    total_out[...] = jnp.broadcast_to(total, total_out.shape)
    states_pass(conv_ref, cum_t, tail_t, state, saved, width, n)
    state_out[...] = state[...].astype(BF16)
    inner_pass(conv_ref, cum_t, row, saved, skip_ref, part, width, n)


def final_kernel(width, n, conv_ref, base_t, incoming, part, gain_ref, out_ref):
    final_pass(conv_ref, base_t, incoming, part, gain_ref, out_ref, width, n)


def vmem():
    return pl.BlockSpec(memory_space=pltpu.VMEM)


def local(tokens, w_xbc, conv_weight, conv_bias, a_log, dt_in, d_skip, norm_gain):
    token_rows = tokens[0]
    rows = token_rows.shape[0]
    heads = a_log.shape[0]
    width = norm_gain.shape[0]
    size = width // heads
    channels = w_xbc.shape[1]
    n = (channels - width) // 2
    blocks = rows // Q
    pad = 16
    count = lax.axis_size("seq")
    rim = lax.ppermute(token_rows[rows - pad :], "seq", [(i, i + 1) for i in range(count - 1)])
    w = lax.all_gather(w_xbc, ("dp", "seq"), axis=0, tiled=True)
    conv_out = project(token_rows, rim, w, conv_weight, conv_bias)
    skip_row = jnp.repeat(d_skip, size)[None, :]
    part, state, total, base_t = pl.pallas_call(
        functools.partial(ssd_kernel, width, n),
        out_shape=(
            jax.ShapeDtypeStruct((rows, width), F32),
            jax.ShapeDtypeStruct((n, width), BF16),
            jax.ShapeDtypeStruct((heads, 128), F32),
            jax.ShapeDtypeStruct((blocks, Q, heads), F32),
        ),
        in_specs=[vmem()] * 4,
        out_specs=(vmem(),) * 4,
        scratch_shapes=[
            pltpu.VMEM((blocks, Q, heads), F32),
            pltpu.VMEM((blocks, heads, Q), F32),
            pltpu.VMEM((blocks, Q, heads), F32),
            pltpu.VMEM((blocks, n, width), BF16),
            pltpu.VMEM((n, width), F32),
        ],
    )(conv_out, dt_in[0], a_log[:, None], skip_row)
    pieces = lax.all_to_all(state.reshape(count, n // count, width), "seq", 0, 0)
    totals = lax.all_gather(total[:, 0], "seq")
    factor = jnp.repeat(jnp.exp2(totals), size, axis=1)
    running = jnp.zeros((n // count, width), F32)
    prefixes = []
    for i in range(count):
        prefixes.append(running.astype(BF16))
        running = factor[i][None, :] * running + pieces[i].astype(F32)
    incoming = lax.all_to_all(jnp.stack(prefixes), "seq", 0, 0).reshape(n, width)
    out = pl.pallas_call(
        functools.partial(final_kernel, width, n),
        out_shape=jax.ShapeDtypeStruct((rows, width), BF16),
        in_specs=[vmem()] * 5,
        out_specs=vmem(),
    )(conv_out, base_t, incoming, part, norm_gain[None, :])
    return out[None]


def solution(mesh):
    return jax.shard_map(
        local,
        mesh=mesh,
        in_specs=(
            P("dp", "seq", None),
            P(("dp", "seq"), None),
            P(),
            P(),
            P(),
            P("dp", None, "seq"),
            P(),
            P(),
        ),
        out_specs=P("dp", "seq", None),
        check_vma=False,
    )
```

```python
import functools
import math

import jax
import jax.numpy as jnp
from jax import lax
from jax.experimental import pallas as pl
from jax.experimental.pallas import tpu as pltpu
from jax.sharding import PartitionSpec as P

Q = 128
RIM = 16
BEHIND = (0, 2, 3, 5, 6)
E1 = 5
E2 = 10
LOG2E = math.log2(math.e)
F32 = jnp.float32
BF16 = jnp.bfloat16
MESH = pl.DeviceIdType.MESH


def dot(a, b, precision=None):
    return lax.dot_general(
        a, b, (((1,), (0,)), ((), ())), precision=precision, preferred_element_type=F32
    )


def vmem():
    return pl.BlockSpec(memory_space=pltpu.VMEM)


def iota(shape, axis):
    return lax.broadcasted_iota(jnp.int32, shape, axis)


def pair_of(left, right):
    return jnp.where(iota((left.shape[0], 128), 1) < 64, left, right)


def four_of(cols):
    return jnp.concatenate([pair_of(cols[0], cols[1]), pair_of(cols[2], cols[3])], axis=1)


def two_of(ref, p):
    return jnp.concatenate([ref[pl.ds(2 * p, 1), :], ref[pl.ds(2 * p + 1, 1), :]], axis=1)


def conv_silu(work, cw, cb, rows, pad):
    taps = cw.shape[0]
    acc = cb
    for k in range(taps):
        acc = acc + cw[k : k + 1, :] * work[pl.ds(pad - (taps - 1) + k, rows), :]
    half = 0.5 * acc
    return half + half * jnp.tanh(half)


def prepare(dt_ref, a_ref, cols, row, dec):
    heads, rows = dt_ref.shape
    groups, blocks = cols.shape[0], cols.shape[1]
    eye = iota((heads, heads), 0) == iota((heads, heads), 1)
    a_row = jnp.broadcast_to(a_ref[...], (heads, heads))
    a_log = jnp.sum(jnp.where(eye, a_row, 0.0), axis=1, keepdims=True)
    v = dt_ref[...]
    dt = jnp.maximum(v, 0.0) + jnp.log1p(jnp.exp(-jnp.abs(v)))
    log_dt = jnp.log2(dt)
    decay = (-LOG2E * jnp.exp(a_log)) * dt
    upper = (iota((Q, Q), 0) <= iota((Q, Q), 1)).astype(F32)
    out = iota((groups * 16, heads), 0)
    head = iota((groups * 16, heads), 1)
    base = jnp.zeros((heads, 1), F32)
    place = [
        ((out // 16 == head // 4) & (lax.rem(out, 16) == 4 * kind + lax.rem(head, 4))).astype(F32)
        for kind in range(3)
    ]
    for c in range(blocks):
        span = slice(c * Q, (c + 1) * Q)
        cum = dot(decay[:, span], upper, lax.Precision.HIGHEST)
        total = cum[:, Q - 1 :]
        row[c] = cum - log_dt[:, span]
        tail = jnp.exp2(total - cum + log_dt[:, span])
        from_start = jnp.exp2(cum + base)
        base = base + total
        mixed = (
            dot(place[0], cum, lax.Precision.HIGHEST)
            + dot(place[1], tail, lax.Precision.HIGHEST)
            + dot(place[2], from_start, lax.Precision.HIGHEST)
        )
        for g in range(groups):
            cols[g, c] = mixed[16 * g : 16 * g + 16].T
    dec[...] = jnp.zeros_like(dec)
    for g in range(groups):
        dec[g : g + 1, 0:16] = cols[g, blocks - 1, Q - 1 : Q, :]


def layer_kernel(width, n, tok_hbm, shard, dt_hbm, cw_hbm, cb_hbm, gain_hbm, a_hbm, skip_hbm, out_hbm,
                 dt_ref, cw_ref, cb_ref, gain_ref, a_ref, own, skip_ref,
                 tok, work, stage, block, w, cols, row, dec, dec_all, keeps, bc, scores, xg, state,
                 sbuf, inbox, outbox, incoming, part, obuf,
                 send, recv, p1s, p1r, p2s, p2r, sems, osem, ssem):
    dp, seq = lax.axis_index("dp"), lax.axis_index("seq")
    x, c = dp // 2, lax.rem(dp, 2)
    z, y = seq // 4, lax.rem(seq, 4)
    rows = tok_hbm.shape[0]
    depth = shard.shape[0]
    pieces = w.shape[0]
    pairs = pieces // 2
    groups = pairs - 1
    blocks = rows // Q
    length = lax.axis_size("seq")

    def at_x(g):
        return {"dp": lax.rem(g, 4) * 2 + c}

    def at_z(g):
        return {"seq": lax.rem(g, 4) * 4 + y}

    def at_y(g):
        return {"seq": z * 4 + lax.rem(g, 4)}

    def at_seq(s):
        return {"seq": lax.rem(s, length)}

    partner = {"dp": 2 * x + 1 - c}

    def remote(src, dst, send_sem, recv_sem, device):
        return pltpu.make_async_remote_copy(
            src_ref=src, dst_ref=dst, send_sem=send_sem, recv_sem=recv_sem,
            device_id=device, device_id_type=MESH)

    load = pltpu.make_async_copy(tok_hbm, tok.at[pl.ds(RIM, rows)], sems.at[0])
    small = [pltpu.make_async_copy(src, dst, ssem.at[k]) for k, (src, dst) in enumerate(
        ((dt_hbm, dt_ref), (a_hbm, a_ref), (shard, own), (cw_hbm, cw_ref), (cb_hbm, cb_ref), (gain_hbm, gain_ref), (skip_hbm, skip_ref)))]
    for one_load in small:
        one_load.start()
    load.start()
    barrier = pltpu.get_barrier_semaphore()
    greet = [at_x(x + 1), at_x(x + 2), at_x(x + 3), partner] + [at_seq(seq + d) for d in range(1, length)]
    for device in greet:
        pl.semaphore_signal(barrier, inc=1, device_id=device, device_id_type=MESH)
    small[0].wait()
    small[1].wait()
    prepare(dt_ref, a_ref, cols, row, dec)
    dec_all[seq] = dec[...]
    pl.semaphore_wait(barrier, len(greet))


    def piece(i, part_):
        return 2 * lax.rem(i + groups, pairs) + part_

    def same(ch, j, ref, device):
        return remote(ref, ref, send.at[ch, j], recv.at[ch, j], device)

    def mine(j):
        return shard.at[:, pl.ds(pl.multiple_of(j * 128, 128), 128)]

    def across(j, d, owner, device):
        return remote(mine(j), stage.at[j, owner], send.at[11 + d, j], recv.at[11 + d, j], device)

    rim = remote(tok_hbm.at[pl.ds(rows - RIM, RIM)], tok.at[pl.ds(0, RIM)],
                 sems.at[1], sems.at[2], at_seq(seq + 1))

    def spread(i, carry):
        for side in (0, 1):
            j = piece(i, side)
            for d in (1, 2, 3):
                across(j, d, y, at_y(y + d)).start()
        return carry

    lax.fori_loop(0, pairs, spread, 0)
    rim.start()

    def axes(side):
        if side == 0:
            return z, x, at_z, at_x
        return x, z, at_x, at_z

    def one(j, side, f):
        f = lax.rem(f, 4)
        return w.at[j, x, c, f] if side == 0 else w.at[j, f, c, z]

    def group(j, side, g, core, half=None):
        g = lax.rem(g, 4)
        if half is None:
            return w.at[j, g, core] if side == 0 else w.at[j, :, core, g]
        span = pl.ds(2 * half, 2)
        return w.at[j, g, core, span] if side == 0 else w.at[j, span, core, g]

    def s1(j, side):
        for d in (1, 2, 3):
            across(j, d, lax.rem(y + 4 - d, 4), partner).wait_recv()
        here = own[:, pl.ds(pl.multiple_of(j * 128, 128), 128)].astype(F32)
        for k in range(4):
            block[k * depth : (k + 1) * depth, :] = jnp.where(y == k, here, stage[j, k].astype(F32))
        w[j, x, c, z] = block[...].astype(BF16)
        f, _, at_f, _ = axes(side)
        same(2, j, one(j, side, f), at_f(f + 2)).start()
        same(0, j, one(j, side, f), at_f(f + 1)).start()
        same(1, j, one(j, side, f), at_f(f + 3)).start()

    def s2(j, side):
        f, g, _, at_g = axes(side)
        for ch, o in ((0, 3), (1, 1), (2, 2)):
            same(ch, j, one(j, side, f + o), partner).wait_recv()
        same(4, j, group(j, side, g, c), at_g(g + 1)).start()
        same(5, j, group(j, side, g, c), at_g(g + 3)).start()
        same(8, j, group(j, side, g, c), partner).start()

    def s3(j, side):
        _, g, _, at_g = axes(side)
        same(4, j, group(j, side, g + 3, c), partner).wait_recv()
        same(6, j, group(j, side, g + 3, c, 0), at_g(g + 1)).start()
        same(9, j, group(j, side, g + 3, c), partner).start()
        same(5, j, group(j, side, g + 1, c), partner).wait_recv()
        same(7, j, group(j, side, g + 1, c, 1), at_g(g + 3)).start()
        same(10, j, group(j, side, g + 1, c), partner).start()

    def s4(j, side):
        _, g, _, _ = axes(side)
        same(6, j, group(j, side, g + 2, c, 0), partner).wait_recv()
        same(7, j, group(j, side, g + 2, c, 1), partner).wait_recv()
        same(11, j, group(j, side, g + 2, c), partner).start()

    def s5(j, side):
        _, g, _, _ = axes(side)
        for ch, o in ((8, 0), (9, 3), (10, 1), (11, 2)):
            same(ch, j, group(j, side, g + o, 1 - c), partner).wait_recv()


    for d in range(1, length):
        remote(dec, dec_all.at[seq], sems.at[3], sems.at[4], at_seq(seq + d)).start()
    for one_load in small[2:]:
        one_load.wait()

    def project(i):
        p = lax.rem(i + groups, pairs)
        span = pl.ds(pl.multiple_of(p * 256, 256), 256)
        weights = jnp.concatenate(
            [w[2 * p].reshape(-1, 128), w[2 * p + 1].reshape(-1, 128)], axis=1)
        work[...] = dot(tok[...], weights).astype(BF16).astype(F32)

        @pl.when(seq == 0)
        def _():
            work[pl.ds(0, RIM), :] = jnp.zeros((RIM, 256), F32)

        return conv_silu(work, cw_ref[:, span], two_of(cb_ref, p), rows, RIM).astype(BF16)

    lower = iota((Q, Q), 0) >= iota((Q, Q), 1)
    left = iota((Q, 128), 1) < 64

    def score(b, carry):
        span = pl.ds(pl.multiple_of(b * Q, Q), Q)
        raw = lax.dot_general(bc[span, n:], bc[span, :n], (((1,), (1,)), ((), ())),
                              preferred_element_type=F32)
        scores[b] = jnp.where(lower, raw, 0.0)
        return carry

    def inner(g):
        state[...] = jnp.zeros_like(state)
        skips = [jnp.full((1, 128), skip_ref[4 * g + k], F32) for k in range(4)]
        skip = four_of(skips)

        def step(b, carry):
            span = pl.ds(pl.multiple_of(b * Q, Q), Q)
            bm, cm = bc[span, :n], bc[span, n:]
            col = cols[g, b]
            xs = xg[span, :]
            xf = xs.astype(F32)
            old = state[...]
            last = col[Q - 1 : Q, :]
            keep = jnp.exp2(four_of([last[:, k : k + 1] for k in range(4)]))
            wx = (xf * four_of([col[:, k : k + 1] for k in range(4, 8)])).astype(BF16)
            state[...] = keep * old + dot(bm.T, wx)
            grow = []
            ys = []
            for q in (0, 1):
                xp = xs[:, 128 * q : 128 * q + 128]
                mixes = []
                own = []
                for k in (2 * q, 2 * q + 1):
                    at = jnp.broadcast_to(col[:, k : k + 1], (Q, 128))
                    spread_ = jnp.where(lower, at - row[b, pl.ds(4 * g + k, 1), :], -jnp.inf)
                    mixes.append((jnp.exp2(spread_) * scores[b]).astype(BF16))
                    own.append(at)
                zero = jnp.zeros_like(xp)
                stack = jnp.concatenate([jnp.where(left, xp, zero), jnp.where(left, zero, xp)], axis=0)
                ys.append(dot(jnp.concatenate(mixes, axis=1), stack))
                grow.append(jnp.exp2(jnp.where(left, own[0], own[1])))
            y_own = jnp.concatenate(ys, axis=1) + skip * xf
            part[g, span, :] = y_own + jnp.concatenate(grow, axis=1) * dot(cm, old.astype(BF16))
            return carry

        lax.fori_loop(0, blocks, step, 0, unroll=True)
        sbuf[g] = state[...].astype(BF16)


    def tile(ref, g, s):
        return ref.at[g, pl.ds(pl.multiple_of((s // 2) * 16, 16), 16),
                      pl.ds(pl.multiple_of(lax.rem(s, 2) * 128, 128), 128)]

    def scatter(g):
        inbox[g, seq] = tile(sbuf, g, seq)[...]
        for d in range(1, length):
            s = lax.rem(seq + d, length)
            remote(tile(sbuf, g, s), inbox.at[g, seq], p1s.at[g], p1r.at[g], at_seq(s)).start()

    def all_but_one(g):
        return inbox.at[g, pl.ds(0, length - 1)]

    def scan(g):
        remote(all_but_one(g), all_but_one(g), p1s.at[g], p1r.at[g], partner).wait_recv()
        run = jnp.zeros((16, 128), F32)
        for s in range(length):
            outbox[g, s] = run.astype(BF16)
            run = keeps[s, pl.ds(g, 1), :] * run + inbox[g, s].astype(F32)
        tile(incoming, g, seq)[...] = outbox[g, seq]
        for d in range(1, length):
            s = lax.rem(seq + d, length)
            remote(outbox.at[g, s], tile(incoming, g, seq), p2s.at[g], p2r.at[g], at_seq(s)).start()

    mean_of = jnp.where((iota((256, 256), 0) // 64) == (iota((256, 256), 1) // 64), 1.0 / 64, 0.0).astype(BF16)

    def put(g):
        return pltpu.make_async_copy(
            obuf.at[g], out_hbm.at[:, pl.ds(pl.multiple_of(g * 256, 256), 256)], osem.at[g])

    def final(g):
        remote(all_but_one(g), all_but_one(g), p2s.at[g], p2r.at[g], partner).wait_recv()
        gain = two_of(gain_ref, g)

        def step(b, carry):
            span = pl.ds(pl.multiple_of(b * Q, Q), Q)
            col = cols[g, b]
            scale = four_of([col[:, k : k + 1] for k in range(8, 12)])
            v = part[g, span, :] + scale * dot(bc[span, n:], incoming[g])
            mean_sq = dot((v * v).astype(BF16), mean_of)
            obuf[g, span, :] = (v * lax.rsqrt(mean_sq + 1e-5) * gain).astype(BF16)
            return carry

        lax.fori_loop(0, blocks, step, 0, unroll=True)
        put(g).start()

    def serve(t, stage_fn, behind):
        i = t - behind

        @pl.when((i >= 0) & (i < pairs))
        def _():
            stage_fn(piece(i, 0), 0)
            stage_fn(piece(i, 1), 1)

    def step(t, carry):
        for k, fn in zip(BEHIND, (s1, s2, s3, s4)):
            serve(t, fn, k)
        i = t - BEHIND[4]

        @pl.when(i == 0)
        def _():
            load.wait()
            rim.wait_recv()
            remote(dec_all.at[pl.ds(0, length - 1)], dec_all.at[pl.ds(0, length - 1)],
                   sems.at[3], sems.at[4], partner).wait_recv()
            right_half = lax.rem(seq, 2) == 1
            for s in range(length):
                decs = dec_all[s]
                keeps[s] = pair_of(jnp.where(right_half, decs[:, 10:11], decs[:, 8:9]),
                                   jnp.where(right_half, decs[:, 11:12], decs[:, 9:10]))
            s5(piece(i, 0), 0)
            s5(piece(i, 1), 1)
            bc[...] = project(i)
            lax.fori_loop(0, blocks, score, 0)

        @pl.when((i > 0) & (i < pairs))
        def _():
            s5(piece(i, 0), 0)
            s5(piece(i, 1), 1)
            xg[...] = project(i)
            inner(i - 1)
            scatter(i - 1)

        @pl.when((i > E1) & (i - 1 - E1 < groups))
        def _():
            scan(i - 1 - E1)

        @pl.when(i > E2)
        def _():
            final(i - 1 - E2)

        return carry

    lax.fori_loop(0, pairs + BEHIND[4] + E2, step, 0)

    def drain(j, side):
        f, g, _, _ = axes(side)
        for d in (1, 2, 3):
            across(j, d, y, partner).wait_send()
        for ch in (0, 1, 2):
            same(ch, j, one(j, side, f), partner).wait_send()
        for ch in (4, 5, 8, 9, 10, 11):
            same(ch, j, group(j, side, g, c), partner).wait_send()
        for ch, half in ((6, 0), (7, 1)):
            same(ch, j, group(j, side, g, c, half), partner).wait_send()

    def end(i, carry):
        drain(2 * i, 0)
        drain(2 * i + 1, 1)
        return carry

    lax.fori_loop(0, pairs, end, 0)

    def end_group(g, carry):
        remote(all_but_one(g), all_but_one(g), p1s.at[g], p1r.at[g], partner).wait_send()
        remote(all_but_one(g), all_but_one(g), p2s.at[g], p2r.at[g], partner).wait_send()
        put(g).wait()
        return carry

    lax.fori_loop(0, groups, end_group, 0)
    rim.wait_send()
    remote(dec_all.at[pl.ds(0, length - 1)], dec_all.at[pl.ds(0, length - 1)],
           sems.at[3], sems.at[4], partner).wait_send()


def local(tokens, w_xbc, conv_weight, conv_bias, a_log, dt_in, d_skip, norm_gain):
    rows, model = tokens.shape[1:]
    heads = a_log.shape[0]
    width = norm_gain.shape[0]
    depth, channels = w_xbc.shape
    n = (channels - width) // 2
    blocks = rows // Q
    pieces = channels // 128
    groups = pieces // 2 - 1
    length = lax.axis_size("seq")
    dma = pltpu.SemaphoreType.DMA
    out = pl.pallas_call(
        functools.partial(layer_kernel, width, n),
        out_shape=jax.ShapeDtypeStruct((rows, width), BF16),
        in_specs=[pl.BlockSpec(memory_space=pltpu.HBM)] * 8,
        out_specs=pl.BlockSpec(memory_space=pl.ANY),
        scratch_shapes=[
            pltpu.VMEM((heads, rows), F32),
            pltpu.VMEM(conv_weight.shape, F32),
            pltpu.VMEM((pieces, 128), F32),
            pltpu.VMEM((width // 128, 128), F32),
            pltpu.VMEM((1, heads), F32),
            pltpu.VMEM((depth, channels), BF16),
            pltpu.SMEM((heads,), F32),
            pltpu.VMEM((rows + RIM, model), BF16),
            pltpu.VMEM((rows + RIM, 256), F32),
            pltpu.VMEM((pieces, 4, depth, 128), BF16),
            pltpu.VMEM((4 * depth, 128), F32),
            pltpu.VMEM((pieces, 4, 2, 4, 4 * depth, 128), BF16),
            pltpu.VMEM((groups, blocks, Q, 16), F32),
            pltpu.VMEM((blocks, heads, Q), F32),
            pltpu.VMEM((16, 128), F32),
            pltpu.VMEM((length, 16, 128), F32),
            pltpu.VMEM((length, 16, 128), F32),
            pltpu.VMEM((rows, 2 * n), BF16),
            pltpu.VMEM((blocks, Q, Q), F32),
            pltpu.VMEM((rows, 256), BF16),
            pltpu.VMEM((n, 256), F32),
            pltpu.VMEM((groups, n, 256), BF16),
            pltpu.VMEM((groups, length, 16, 128), BF16),
            pltpu.VMEM((groups, length, 16, 128), BF16),
            pltpu.VMEM((groups, n, 256), BF16),
            pltpu.VMEM((groups, rows, 256), F32),
            pltpu.VMEM((groups, rows, 256), BF16),
            dma((15, pieces)),
            dma((15, pieces)),
            dma((groups,)),
            dma((groups,)),
            dma((groups,)),
            dma((groups,)),
            dma((5,)),
            dma((groups,)),
            dma((7,)),
        ],
        compiler_params=pltpu.CompilerParams(collective_id=0, has_side_effects=True, vmem_limit_bytes=48 * 2**20),
    )(*[pltpu.with_memory_space_constraint(v, pltpu.HBM) for v in (
        tokens[0], w_xbc, dt_in[0], conv_weight, conv_bias.reshape(-1, 128), norm_gain.reshape(-1, 128),
        a_log[None, :], d_skip)])
    return out[None]


def solution(mesh):
    return jax.shard_map(
        local,
        mesh=mesh,
        in_specs=(
            P("dp", "seq", None),
            P(("dp", "seq"), None),
            P(),
            P(),
            P(),
            P("dp", None, "seq"),
            P(),
            P(),
        ),
        out_specs=P("dp", "seq", None),
        check_vma=False,
    )
```
